512 devices in a mesh: ingest: 32 (over x, y), section: 16 (over z, core).
Axes of the slice: x: 4, y: 8, z: 8, core: 2. Of those that a mesh axis runs over, the one named last changes fastest.
Arguments:
- txn_feats: bfloat16 [131072, 2048], P(('ingest', 'section')), may hold values from -6 to 6
- txn_seg: int32 [512, 256], P(('ingest', 'section')), may hold values from 0 to 255, as said below
- seg_row: int32 [512, 256], P(('ingest', 'section')), may hold values from 0 to 15, as said below
- send_counts: int32 [512, 32], P(('ingest', 'section')), may hold values from 0 to 8, as said below
- gains: float32 [16, 2048], P('section'), may hold values from 0.5 to 1.5
- tower_w: bfloat16 [16, 2048, 2048], P('section', 'ingest'), may hold values from -0.125 to 0.125
Outputs:
- card_embed: bfloat16 [8192, 2048], P(('ingest', 'section'))
The draws below stay inside these ranges and needn't reach their ends.
Inputs may be any that keep to these rules, and one draw needn't show every extreme that they name: Each row of send_counts is at most 8 everywhere; in each section index one owner index gets exactly 8 from every device of that section; device 0 sends exactly 8 to every owner. Within a device's row txn_seg never falls, starts at 0 and ends at that device's sum of send_counts minus one. `seg_row`: the segments that one device sends to one owner name different card rows.
All inputs are finite; a program needn't handle non-finite values.
Results may differ from the reference program's by a relative error of at most 0.012.
Values may be sent and summed in bfloat16 or wider, within the bound.
No kernel may reach another device: no remote copies, remote signals or barrier semaphores. Data moves between devices by JAX's collectives and lax.ppermute only.
A program may use at most 64 MiB of HBM per device.

```python
import jax
import jax.numpy as jnp
from jax import lax

D = 2048
TXN_DEV = 256
CARD_DEV = 16
CAP = 8
TXN = 131072
LAYERS = 16
N_INGEST = 32
N_SECTION = 16


def make_lists(key):
    base = jax.random.fold_in(key, 7)
    key_counts, key_hot, key_seg, key_perm, key_fill = jax.random.split(base, 5)
    devs = N_INGEST * N_SECTION
    slots = N_INGEST * CAP
    counts = jax.random.randint(key_counts, (devs, N_INGEST), 0, CAP + 1).astype(jnp.int32)
    hot = jax.random.randint(key_hot, (N_SECTION,), 0, N_INGEST).astype(jnp.int32)
    hot_dev = hot[jnp.arange(devs) % N_SECTION]
    owners = jnp.arange(N_INGEST, dtype=jnp.int32)
    counts = jnp.where(owners[None, :] == hot_dev[:, None], CAP, counts).astype(jnp.int32)
    first_dev = (jnp.arange(devs, dtype=jnp.int32) == 0)[:, None]
    counts = jnp.where(first_dev, CAP, counts).astype(jnp.int32)
    ends = jnp.cumsum(counts, axis=1).astype(jnp.int32)
    starts = ends - counts
    used = ends[:, -1]
    raw = jax.random.randint(key_seg, (devs, TXN_DEV), 0, 1 << 20).astype(jnp.int32)
    segs = jnp.sort(raw % used[:, None], axis=1).astype(jnp.int32)
    segs = segs.at[:, 0].set(0)
    segs = segs.at[:, -1].set(used - 1).astype(jnp.int32)
    table = jnp.tile(jnp.arange(CARD_DEV, dtype=jnp.int32)[None, :], (devs * N_INGEST, 1))
    perm = jax.random.permutation(key_perm, table, axis=1, independent=True).reshape(devs, N_INGEST * CARD_DEV)
    g = jnp.arange(slots, dtype=jnp.int32)
    owner = jnp.sum((g[None, :, None] >= ends[:, None, :]).astype(jnp.int32), axis=2)
    owner = jnp.minimum(owner, N_INGEST - 1)
    rank = g[None, :] - jnp.take_along_axis(starts, owner, axis=1)
    rank = jnp.clip(rank, 0, CARD_DEV - 1)
    picked = jnp.take_along_axis(perm, owner * CARD_DEV + rank, axis=1)
    filler = jax.random.randint(key_fill, (devs, slots), 0, CARD_DEV).astype(jnp.int32)
    rows = jnp.where(g[None, :] < used[:, None], picked, filler).astype(jnp.int32)
    return (counts, segs, rows)


def draw_txn_seg(key, part):
    return make_lists(key)[1]


def draw_seg_row(key, part):
    return make_lists(key)[2]


def draw_send_counts(key, part):
    return make_lists(key)[0]


def block_levels(own_key, extent, cuts, low, top_value):
    factor_of, own = 1.0, jax.random.fold_in(own_key, 6)
    for dim, blocks in cuts:
        draws = jnp.exp(jax.random.uniform(jax.random.fold_in(own, dim), (blocks,), jnp.float32, low / len(cuts), top_value / len(cuts)))
        factor_of = factor_of * jnp.repeat(draws, extent[dim] // blocks).reshape([-1 if axis == dim else 1 for axis in range(len(extent))])
    return factor_of


def normal_values(key, extent, spread, most, pieces=(), held_as=jnp.bfloat16):
    drawn = jax.random.normal(key, extent, jnp.float32) * spread
    if len(pieces) > 0:
        drawn = block_levels(key, extent, pieces, -0.22, 0.18) * drawn
    return jnp.clip(drawn, min=-most, max=most).astype(held_as)


def setup_inputs(seed: int = 0) -> dict:
    key_of = jax.random.split(jax.random.key(seed), 7)
    return {
        "txn_feats": normal_values(key_of[0], (TXN, D), 1.0, 6.0, ((0, 512),)),
        "txn_seg": draw_txn_seg(jax.random.fold_in(key_of[6], 71), 0),
        "seg_row": draw_seg_row(jax.random.fold_in(key_of[6], 71), 0),
        "send_counts": draw_send_counts(jax.random.fold_in(key_of[6], 71), 0),
        "gains": jnp.clip(1.0 + 0.1 * jax.random.normal(key_of[4], (LAYERS, D), jnp.float32), 0.5, 1.5),
        "tower_w": normal_values(key_of[5], (LAYERS, D, D), D ** -0.5, 0.125, ((0, 16), (1, 32))),
    }


def tower_layer(x, gain, weight):
    u = x.astype(jnp.float32)
    mean_sq = lax.optimization_barrier(jnp.mean(u * u, axis=-1, keepdims=True))
    normed = (u * lax.rsqrt(mean_sq + 1e-05) * gain).astype(jnp.bfloat16)
    y = jnp.dot(normed.astype(jnp.float32), weight.astype(jnp.float32), precision=lax.Precision.HIGHEST)
    return (u + jax.nn.silu(y)).astype(jnp.bfloat16)

def reference(txn_feats, txn_seg, seg_row, send_counts, gains, tower_w):
    devs = N_INGEST * N_SECTION
    slots = N_INGEST * CAP
    feats = txn_feats.reshape(devs, TXN_DEV, D)
    slot_ids = jnp.arange(slots, dtype=jnp.int32)

    def pool(d, table):
        part = lax.dynamic_index_in_dim(feats, d, 0, keepdims=False).astype(jnp.float32)
        seg = lax.dynamic_index_in_dim(txn_seg, d, 0, keepdims=False)
        rows = lax.dynamic_index_in_dim(seg_row, d, 0, keepdims=False)
        counts = lax.dynamic_index_in_dim(send_counts, d, 0, keepdims=False)
        onehot = (slot_ids[:, None] == seg[None, :]).astype(jnp.float32)
        sums = jnp.dot(onehot, part, precision=lax.Precision.HIGHEST).astype(jnp.bfloat16)
        sums = lax.optimization_barrier(sums).astype(jnp.float32)
        ends = jnp.cumsum(counts).astype(jnp.int32)
        owner = lax.optimization_barrier(jnp.sum((slot_ids[:, None] >= ends[None, :]).astype(jnp.int32), axis=1))
        valid = slot_ids < ends[-1]
        owner = jnp.minimum(owner, N_INGEST - 1)
        section_idx = (d % N_SECTION).astype(jnp.int32)
        target = ((owner * N_SECTION + section_idx) * CARD_DEV + rows).astype(jnp.int32)
        target = jnp.where(valid, target, 0).astype(jnp.int32)
        return table.at[target].add(sums * valid[:, None].astype(jnp.float32))
    table = lax.fori_loop(0, devs, pool, jnp.zeros((devs * CARD_DEV, D), jnp.float32))
    x = table.astype(jnp.bfloat16)
    for layer in range(N_SECTION):
        x = tower_layer(x, gains[layer], tower_w[layer])
    return x
```

```python
import functools

import jax
import jax.numpy as jnp
from jax import lax
from jax.experimental import pallas as pl
from jax.experimental.pallas import tpu as pltpu
from jax.sharding import Mesh, PartitionSpec as P

CARD_DEV = 16
X, Y, Z, C = 4, 8, 8, 2
DEVICES = ("x", "y", "z", "c")
LANES = 128
BLOCK = 512
VMEM = pltpu.MemorySpace.VMEM
SMEM = pltpu.MemorySpace.SMEM
MIB = 1024 * 1024


def pool_kernel(counts_ref, seg_ref, rows_ref, feats_ref, out_ref, *, cap):
    owners = counts_ref.shape[1]
    slots = rows_ref.shape[1]
    txns, width = feats_ref.shape
    counts = counts_ref[...]
    below = lax.broadcasted_iota(jnp.int32, (owners, owners), 0)
    across = lax.broadcasted_iota(jnp.int32, (owners, owners), 1)
    counts_all = jnp.broadcast_to(counts, (owners, owners))
    starts_col = jnp.sum(jnp.where(across < below, counts_all, 0), axis=1, keepdims=True)
    counts_col = jnp.sum(jnp.where(across == below, counts_all, 0), axis=1, keepdims=True)
    ends_col = starts_col + counts_col
    starts_row = jnp.sum(
        jnp.where(below < across, jnp.broadcast_to(counts_col, (owners, owners)), 0),
        axis=0,
        keepdims=True,
    )
    seg = seg_ref[...]
    ids = lax.broadcasted_iota(jnp.int32, (owners, txns), 0)
    owner = jnp.sum((seg >= ends_col).astype(jnp.int32), axis=0, keepdims=True)
    start = jnp.sum(jnp.where(ids == owner, starts_col, 0), axis=0, keepdims=True)
    target = owner * cap + seg - start
    slot = lax.broadcasted_iota(jnp.int32, (slots, txns), 0)
    place = (slot == target).astype(jnp.float32).astype(jnp.bfloat16)
    part = jnp.dot(place, feats_ref[...], preferred_element_type=jnp.float32)
    out_ref[:, :width] = part.astype(jnp.bfloat16)
    slot_col = lax.broadcasted_iota(jnp.int32, (slots, owners), 0)
    owner_row = lax.broadcasted_iota(jnp.int32, (slots, owners), 1)
    mine = (slot_col // cap) == owner_row
    slot_start = jnp.sum(jnp.where(mine, starts_row, 0), axis=1, keepdims=True)
    slot_count = jnp.sum(jnp.where(mine, counts, 0), axis=1, keepdims=True)
    rank = lax.broadcasted_iota(jnp.int32, (slots, 1), 0) % cap
    named = lax.broadcasted_iota(jnp.int32, (slots, slots), 1) == slot_start + rank
    row = jnp.sum(jnp.where(named, rows_ref[...], 0), axis=1, keepdims=True)
    label = jnp.where(rank < slot_count, row, -1)
    out_ref[:, width:] = jnp.broadcast_to(
        label.astype(jnp.float32), (slots, LANES)
    ).astype(jnp.bfloat16)


def pool(counts, seg, rows, feats):
    slots = rows.shape[1]
    width = feats.shape[1]
    cap = slots // counts.shape[1]
    return pl.pallas_call(
        functools.partial(pool_kernel, cap=cap),
        out_shape=jax.ShapeDtypeStruct((slots, width + LANES), jnp.bfloat16),
        in_specs=[pl.BlockSpec(memory_space=VMEM)] * 4,
        out_specs=pl.BlockSpec(memory_space=VMEM),
        compiler_params=pltpu.CompilerParams(vmem_limit_bytes=24 * MIB),
        name="pool",
    )(counts, seg, rows, feats)


def pick_kernel(got_ref, out_ref, *, cards, cap, groups):
    senders, slots, wide = got_ref.shape
    width = wide - LANES
    total = senders * slots
    got = got_ref[...].reshape(total, wide)
    label = got[:, width : width + 1].astype(jnp.float32).astype(jnp.int32)
    slot = lax.broadcasted_iota(jnp.int32, (total, 1), 0)
    card = jnp.where(label >= 0, ((slot // cap) % groups) * cards + label, -1)
    ids = lax.broadcasted_iota(jnp.int32, (total, groups * cards), 1)
    hot = (ids == card).astype(jnp.float32).astype(jnp.bfloat16)
    out = lax.dot_general(
        hot, got[:, :width], (((0,), (0,)), ((), ())), preferred_element_type=jnp.float32
    )
    out_ref[...] = out.astype(jnp.bfloat16)


def pick(got, cap, groups):
    width = got.shape[2] - LANES
    out = pl.pallas_call(
        functools.partial(pick_kernel, cards=CARD_DEV, cap=cap, groups=groups),
        out_shape=jax.ShapeDtypeStruct((groups * CARD_DEV, width), jnp.bfloat16),
        in_specs=[pl.BlockSpec(memory_space=VMEM)],
        out_specs=pl.BlockSpec(memory_space=VMEM),
        compiler_params=pltpu.CompilerParams(vmem_limit_bytes=24 * MIB),
        name="pick",
    )(got)
    return out.reshape(groups, CARD_DEV, width)


def load_kernel(gathered_ref, out_ref, sem):
    blocks, layers, rows, width = gathered_ref.shape
    copies = [
        pltpu.make_async_copy(
            gathered_ref.at[b, layer], out_ref.at[layer, pl.ds(b * rows, rows)], sem.at[b, layer]
        )
        for b in range(blocks)
        for layer in range(layers)
    ]
    for copy in copies:
        copy.start()
    for copy in copies:
        copy.wait()


def load_weights(gathered):
    blocks, layers, rows, width = gathered.shape
    return pl.pallas_call(
        load_kernel,
        out_shape=pltpu.VMEM((layers, blocks * rows, width), jnp.bfloat16),
        in_specs=[pl.BlockSpec(memory_space=pl.ANY)],
        out_specs=pl.BlockSpec(memory_space=VMEM),
        scratch_shapes=[pltpu.SemaphoreType.DMA((blocks, layers))],
        compiler_params=pltpu.CompilerParams(vmem_limit_bytes=20 * MIB),
        name="load_weights",
    )(gathered)


def stage_kernel(position_ref, x_ref, gain_ref, weight_ref, out_ref, normed_ref, *, step):
    active = (step >= position_ref[0]) & (step < position_ref[0] + Z)
    width = x_ref.shape[1]
    out_ref[...] = x_ref[...]

    @pl.when(active)
    def _():
        def layer_of(layer, carry):
            u = out_ref[...].astype(jnp.float32)
            mean_sq = jnp.mean(u * u, axis=-1, keepdims=True)
            normed = u * lax.rsqrt(mean_sq + 1e-05) * gain_ref[pl.ds(layer, 1), :]
            normed_ref[...] = normed.astype(jnp.bfloat16)

            def columns_of(block, carry):
                columns = pl.ds(pl.multiple_of(block * BLOCK, BLOCK), BLOCK)
                y = jnp.dot(
                    normed_ref[...],
                    weight_ref[layer, :, columns],
                    preferred_element_type=jnp.float32,
                )
                u = out_ref[:, columns].astype(jnp.float32)
                out_ref[:, columns] = (u + y / (1.0 + jnp.exp(-y))).astype(jnp.bfloat16)
                return carry

            return lax.fori_loop(0, width // BLOCK, columns_of, carry)

        lax.fori_loop(0, weight_ref.shape[0], layer_of, 0)


def stage(position, x, gain, weight, step):
    return pl.pallas_call(
        functools.partial(stage_kernel, step=step),
        out_shape=jax.ShapeDtypeStruct(x.shape, x.dtype),
        in_specs=[pl.BlockSpec(memory_space=SMEM)] + [pl.BlockSpec(memory_space=VMEM)] * 3,
        out_specs=pl.BlockSpec(memory_space=VMEM),
        scratch_shapes=[pltpu.VMEM(x.shape, jnp.bfloat16)],
        compiler_params=pltpu.CompilerParams(vmem_limit_bytes=24 * MIB),
        name="stage",
    )(position, x, gain, weight)


def body(txn_feats, txn_seg, seg_row, send_counts, gains, tower_w):
    width = txn_feats.shape[1]
    slots = seg_row.shape[1]
    cap = slots // (X * Y)
    gathered = lax.all_gather(tower_w[0], ("x", "y", "c"), axis=0, tiled=False)
    gain = lax.all_gather(gains[0], "c", axis=0, tiled=False)
    buffer = pool(send_counts, txn_seg, seg_row, txn_feats)
    got = lax.all_to_all(buffer.reshape(X, Y * cap, width + LANES), "x", 0, 0, tiled=True)
    dense = pick(got, cap, Y)
    shares = lax.all_to_all(dense, "y", 0, 0, tiled=True)
    pooled = jnp.sum(shares.astype(jnp.float32), axis=0).astype(jnp.bfloat16)
    weight = load_weights(gathered.reshape(X * Y, C, *tower_w.shape[1:]))
    position = lax.axis_index("z").reshape(1)
    x = pooled
    for step in range(2 * Z):
        if step < 2 * Z - 1:
            x = stage(position, x, gain, weight, step)
        x = lax.ppermute(x, "z", [(i, (i + 1) % Z) for i in range(Z)])
    return x


def solution(mesh):
    split = Mesh(mesh.devices.reshape(X, Y, Z, C), DEVICES)
    in_specs = (
        P(DEVICES, None),
        P(DEVICES, None),
        P(DEVICES, None),
        P(DEVICES, None),
        P(("z", "c"), None),
        P(("z", "c"), ("x", "y"), None),
    )
    return jax.shard_map(
        body, mesh=split, in_specs=in_specs, out_specs=P(DEVICES, None), check_vma=False
    )
```

```python
import functools

import jax
import jax.numpy as jnp
from jax import lax
from jax.experimental import pallas as pl
from jax.experimental.pallas import tpu as pltpu
from jax.sharding import Mesh, PartitionSpec as P

CARD_DEV = 16
X, Y, Z, C = 4, 8, 8, 2
DEVICES = ("x", "y", "z", "c")
LANES = 128
BLOCK = 1024
TURNS = 2
BATCH = 2 * CARD_DEV
VMEM = pltpu.MemorySpace.VMEM
SMEM = pltpu.MemorySpace.SMEM
MIB = 1024 * 1024


def pool_kernel(counts_ref, seg_ref, rows_ref, feats_ref, out_ref, *, cap):
    owners = counts_ref.shape[1]
    slots = rows_ref.shape[1]
    txns, width = feats_ref.shape
    counts = counts_ref[...]
    below = lax.broadcasted_iota(jnp.int32, (owners, owners), 0)
    across = lax.broadcasted_iota(jnp.int32, (owners, owners), 1)
    counts_all = jnp.broadcast_to(counts, (owners, owners))
    starts_col = jnp.sum(jnp.where(across < below, counts_all, 0), axis=1, keepdims=True)
    counts_col = jnp.sum(jnp.where(across == below, counts_all, 0), axis=1, keepdims=True)
    ends_col = starts_col + counts_col
    starts_row = jnp.sum(
        jnp.where(below < across, jnp.broadcast_to(counts_col, (owners, owners)), 0),
        axis=0,
        keepdims=True,
    )
    seg = seg_ref[...]
    ids = lax.broadcasted_iota(jnp.int32, (owners, txns), 0)
    owner = jnp.sum((seg >= ends_col).astype(jnp.int32), axis=0, keepdims=True)
    start = jnp.sum(jnp.where(ids == owner, starts_col, 0), axis=0, keepdims=True)
    target = owner * cap + seg - start
    slot = lax.broadcasted_iota(jnp.int32, (slots, txns), 0)
    place = (slot == target).astype(jnp.float32).astype(jnp.bfloat16)
    part = jnp.dot(place, feats_ref[...], preferred_element_type=jnp.float32)
    out_ref[:, :width] = part.astype(jnp.bfloat16)
    slot_col = lax.broadcasted_iota(jnp.int32, (slots, owners), 0)
    owner_row = lax.broadcasted_iota(jnp.int32, (slots, owners), 1)
    mine = (slot_col // cap) == owner_row
    slot_start = jnp.sum(jnp.where(mine, starts_row, 0), axis=1, keepdims=True)
    slot_count = jnp.sum(jnp.where(mine, counts, 0), axis=1, keepdims=True)
    rank = lax.broadcasted_iota(jnp.int32, (slots, 1), 0) % cap
    named = lax.broadcasted_iota(jnp.int32, (slots, slots), 1) == slot_start + rank
    row = jnp.sum(jnp.where(named, rows_ref[...], 0), axis=1, keepdims=True)
    label = jnp.where(rank < slot_count, row, -1)
    out_ref[:, width:] = jnp.broadcast_to(
        label.astype(jnp.float32), (slots, LANES)
    ).astype(jnp.bfloat16)


def pool(counts, seg, rows, feats):
    slots = rows.shape[1]
    width = feats.shape[1]
    cap = slots // counts.shape[1]
    return pl.pallas_call(
        functools.partial(pool_kernel, cap=cap),
        out_shape=jax.ShapeDtypeStruct((slots, width + LANES), jnp.bfloat16),
        in_specs=[pl.BlockSpec(memory_space=VMEM)] * 4,
        out_specs=pl.BlockSpec(memory_space=VMEM),
        compiler_params=pltpu.CompilerParams(vmem_limit_bytes=24 * MIB),
        name="pool",
    )(counts, seg, rows, feats)


def pick_kernel(got_ref, out_ref, *, cards, cap, groups):
    senders, slots, wide = got_ref.shape
    width = wide - LANES
    total = senders * slots
    got = got_ref[...].reshape(total, wide)
    label = got[:, width : width + 1].astype(jnp.float32).astype(jnp.int32)
    slot = lax.broadcasted_iota(jnp.int32, (total, 1), 0)
    card = jnp.where(label >= 0, ((slot // cap) % groups) * cards + label, -1)
    ids = lax.broadcasted_iota(jnp.int32, (total, groups * cards), 1)
    hot = (ids == card).astype(jnp.float32).astype(jnp.bfloat16)
    out = lax.dot_general(
        hot, got[:, :width], (((0,), (0,)), ((), ())), preferred_element_type=jnp.float32
    )
    out_ref[...] = out.astype(jnp.bfloat16)


def pick(got, cap, groups):
    width = got.shape[2] - LANES
    out = pl.pallas_call(
        functools.partial(pick_kernel, cards=CARD_DEV, cap=cap, groups=groups),
        out_shape=jax.ShapeDtypeStruct((groups * CARD_DEV, width), jnp.bfloat16),
        in_specs=[pl.BlockSpec(memory_space=VMEM)],
        out_specs=pl.BlockSpec(memory_space=VMEM),
        compiler_params=pltpu.CompilerParams(vmem_limit_bytes=24 * MIB),
        name="pick",
    )(got)
    return out.reshape(groups, CARD_DEV, width)


def load_kernel(gathered_ref, out_ref, sem):
    blocks, layers, rows, width = gathered_ref.shape
    copies = [
        pltpu.make_async_copy(
            gathered_ref.at[b, layer], out_ref.at[layer, pl.ds(b * rows, rows)], sem.at[b, layer]
        )
        for b in range(blocks)
        for layer in range(layers)
    ]
    for copy in copies:
        copy.start()
    for copy in copies:
        copy.wait()


def load_weights(gathered):
    blocks, layers, rows, width = gathered.shape
    return pl.pallas_call(
        load_kernel,
        out_shape=pltpu.VMEM((layers, blocks * rows, width), jnp.bfloat16),
        in_specs=[pl.BlockSpec(memory_space=pltpu.MemorySpace.HBM)],
        out_specs=pl.BlockSpec(memory_space=VMEM),
        scratch_shapes=[pltpu.SemaphoreType.DMA((blocks, layers))],
        compiler_params=pltpu.CompilerParams(vmem_limit_bytes=20 * MIB),
        name="load_weights",
    )(gathered)


def run_layers(out_ref, gain_ref, weight_ref, normed_ref):
    width = out_ref.shape[1]

    def layer_of(layer, carry):
        u = out_ref[...].astype(jnp.float32)
        mean_sq = jnp.mean(u * u, axis=-1, keepdims=True)
        normed = u * lax.rsqrt(mean_sq + 1e-05) * gain_ref[pl.ds(layer, 1), :]
        normed_ref[...] = normed.astype(jnp.bfloat16)

        def columns_of(block, carry):
            columns = pl.ds(pl.multiple_of(block * BLOCK, BLOCK), BLOCK)
            y = jnp.dot(
                normed_ref[...],
                weight_ref[layer, :, columns],
                preferred_element_type=jnp.float32,
            )
            u = out_ref[:, columns].astype(jnp.float32)
            out_ref[:, columns] = (u + y / (1.0 + jnp.exp(-y))).astype(jnp.bfloat16)
            return carry

        return lax.fori_loop(0, width // BLOCK, columns_of, carry)

    lax.fori_loop(0, weight_ref.shape[0], layer_of, 0)


def stage_kernel(position_ref, *refs, step, fresh):
    *sources, gain_ref, weight_ref, out_ref, normed_ref = refs
    age = step - position_ref[0]

    @pl.when((age >= 0) & (age < TURNS))
    def _():
        if fresh is None:
            out_ref[...] = sources[-1][...]
        elif len(sources) == 1:
            out_ref[...] = sources[0][fresh : fresh + BATCH, :]
        else:
            first = position_ref[0] == 0

            @pl.when(first)
            def _():
                out_ref[...] = sources[0][fresh : fresh + BATCH, :]

            @pl.when(jnp.logical_not(first))
            def _():
                out_ref[...] = sources[1][...]

        run_layers(out_ref, gain_ref, weight_ref, normed_ref)


def stage(position, queue, came, gain, weight, step, fresh):
    sources = [a for a in (queue if fresh is not None else None, came) if a is not None]
    shape = (BATCH, gain.shape[1])
    return pl.pallas_call(
        functools.partial(stage_kernel, step=step, fresh=fresh),
        out_shape=jax.ShapeDtypeStruct(shape, jnp.bfloat16),
        in_specs=[pl.BlockSpec(memory_space=SMEM)]
        + [pl.BlockSpec(memory_space=VMEM)] * (len(sources) + 2),
        out_specs=pl.BlockSpec(memory_space=VMEM),
        scratch_shapes=[pltpu.VMEM(shape, jnp.bfloat16)],
        compiler_params=pltpu.CompilerParams(vmem_limit_bytes=24 * MIB),
        name="stage",
    )(position, *sources, gain, weight)


def choose_kernel(position_ref, *refs, cases):
    out_ref = refs[-1]
    for homes, which, row in cases:
        mine = position_ref[0] == homes[0]
        for home in homes[1:]:
            mine = mine | (position_ref[0] == home)

        @pl.when(mine)
        def _():
            out_ref[...] = refs[which][row : row + CARD_DEV, :]


def choose(position, arrays, cases):
    return pl.pallas_call(
        functools.partial(choose_kernel, cases=cases),
        out_shape=jax.ShapeDtypeStruct((CARD_DEV, arrays[0].shape[1]), jnp.bfloat16),
        in_specs=[pl.BlockSpec(memory_space=SMEM)]
        + [pl.BlockSpec(memory_space=VMEM)] * len(arrays),
        out_specs=pl.BlockSpec(memory_space=VMEM),
        compiler_params=pltpu.CompilerParams(vmem_limit_bytes=8 * MIB),
        name="choose",
    )(position, *arrays)


def collect(pooled):
    pairs = jnp.concatenate([lax.ppermute(pooled, "z", [(7, 0), (1, 2), (3, 4), (5, 6)]), pooled])
    fours = jnp.concatenate([pairs, lax.ppermute(pairs, "z", [(2, 0), (6, 4)])])
    return jnp.concatenate([fours, lax.ppermute(fours, "z", [(4, 0)])])


def tower(position, queue, gain, weight):
    streams = [
        dict(fresh=(2 * CARD_DEV, 6 * CARD_DEV), home=(2, 6)),
        dict(fresh=(4 * CARD_DEV, 0), home=(4, 0)),
    ]
    came = [None, None]
    kept = [[], []]
    done = [None, None]
    for step in range(Z - 1 + TURNS):
        for s, stream in enumerate(streams):
            fresh = stream["fresh"][step] if step < TURNS else None
            done[s] = stage(position, queue, came[s], gain, weight, step, fresh)
            moves = [(z, z + 1) for z in range(Z - 1) if 0 <= step - z < TURNS]
            if step >= Z - 1:
                moves.append((Z - 1, stream["home"][step - Z + 1]))
            came[s] = lax.ppermute(done[s], "z", moves)
            if step >= Z - 1:
                kept[s].append(came[s])
    (two, six), (four, zero) = kept
    lent = choose(position, [two, four, six], (((2,), 0, 0), ((4,), 1, 0), ((6,), 2, 0)))
    lent = lax.ppermute(lent, "z", [(2, 1), (4, 3), (6, 5)])
    cases = (
        ((2,), 0, CARD_DEV),
        ((4,), 1, CARD_DEV),
        ((6,), 2, CARD_DEV),
        ((0,), 3, CARD_DEV),
        ((1, 3, 5), 4, 0),
        ((7,), 5, 0),
    )
    return choose(position, [two, four, six, zero, lent, done[1]], cases)


def body(txn_feats, txn_seg, seg_row, send_counts, gains, tower_w):
    width = txn_feats.shape[1]
    slots = seg_row.shape[1]
    cap = slots // (X * Y)
    gathered = lax.all_gather(tower_w[0], ("x", "y", "c"), axis=0, tiled=False)
    gain = lax.all_gather(gains[0], "c", axis=0, tiled=False)
    buffer = pool(send_counts, txn_seg, seg_row, txn_feats)
    got = lax.all_to_all(buffer.reshape(X, Y * cap, width + LANES), "x", 0, 0, tiled=True)
    dense = pick(got, cap, Y)
    shares = lax.all_to_all(dense, "y", 0, 0, tiled=True)
    pooled = jnp.sum(shares.astype(jnp.float32), axis=0).astype(jnp.bfloat16)
    queue = collect(pooled)
    weight = load_weights(gathered.reshape(X * Y, C, *tower_w.shape[1:]))
    position = lax.axis_index("z").reshape(1)
    return tower(position, queue, gain, weight)


def solution(mesh):
    split = Mesh(mesh.devices.reshape(X, Y, Z, C), DEVICES)
    in_specs = (
        P(DEVICES, None),
        P(DEVICES, None),
        P(DEVICES, None),
        P(DEVICES, None),
        P(("z", "c"), None),
        P(("z", "c"), ("x", "y"), None),
    )
    return jax.shard_map(
        body, mesh=split, in_specs=in_specs, out_specs=P(DEVICES, None), check_vma=False
    )
```

```python
import functools

import jax
import jax.numpy as jnp
from jax import lax
from jax.experimental import pallas as pl
from jax.experimental.pallas import tpu as pltpu
from jax.sharding import Mesh, PartitionSpec as P

CARD_DEV = 16
X, Y, Z, C = 4, 8, 8, 2
DEVICES = ("x", "y", "z", "c")
LANES = 128
BLOCK = 1024
TURNS = 2
BATCH = 2 * CARD_DEV
VMEM = pltpu.MemorySpace.VMEM
SMEM = pltpu.MemorySpace.SMEM
MIB = 1024 * 1024


def pool_kernel(counts_ref, seg_ref, rows_ref, feats_ref, out_ref, *, cap):
    owners = counts_ref.shape[1]
    slots = rows_ref.shape[1]
    txns, width = feats_ref.shape
    counts = counts_ref[...]
    below = lax.broadcasted_iota(jnp.int32, (owners, owners), 0)
    across = lax.broadcasted_iota(jnp.int32, (owners, owners), 1)
    counts_all = jnp.broadcast_to(counts, (owners, owners))
    starts_col = jnp.sum(jnp.where(across < below, counts_all, 0), axis=1, keepdims=True)
    counts_col = jnp.sum(jnp.where(across == below, counts_all, 0), axis=1, keepdims=True)
    ends_col = starts_col + counts_col
    starts_row = jnp.sum(
        jnp.where(below < across, jnp.broadcast_to(counts_col, (owners, owners)), 0),
        axis=0,
        keepdims=True,
    )
    seg = seg_ref[...]
    ids = lax.broadcasted_iota(jnp.int32, (owners, txns), 0)
    owner = jnp.sum((seg >= ends_col).astype(jnp.int32), axis=0, keepdims=True)
    start = jnp.sum(jnp.where(ids == owner, starts_col, 0), axis=0, keepdims=True)
    target = owner * cap + seg - start
    slot = lax.broadcasted_iota(jnp.int32, (slots, txns), 0)
    place = (slot == target).astype(jnp.float32).astype(jnp.bfloat16)
    part = jnp.dot(place, feats_ref[...], preferred_element_type=jnp.float32)
    out_ref[:, :width] = part.astype(jnp.bfloat16)
    slot_col = lax.broadcasted_iota(jnp.int32, (slots, owners), 0)
    owner_row = lax.broadcasted_iota(jnp.int32, (slots, owners), 1)
    mine = (slot_col // cap) == owner_row
    slot_start = jnp.sum(jnp.where(mine, starts_row, 0), axis=1, keepdims=True)
    slot_count = jnp.sum(jnp.where(mine, counts, 0), axis=1, keepdims=True)
    rank = lax.broadcasted_iota(jnp.int32, (slots, 1), 0) % cap
    named = lax.broadcasted_iota(jnp.int32, (slots, slots), 1) == slot_start + rank
    row = jnp.sum(jnp.where(named, rows_ref[...], 0), axis=1, keepdims=True)
    label = jnp.where(rank < slot_count, row, -1)
    out_ref[:, width:] = jnp.broadcast_to(
        label.astype(jnp.float32), (slots, LANES)
    ).astype(jnp.bfloat16)


def pool(counts, seg, rows, feats):
    slots = rows.shape[1]
    width = feats.shape[1]
    cap = slots // counts.shape[1]
    return pl.pallas_call(
        functools.partial(pool_kernel, cap=cap),
        out_shape=jax.ShapeDtypeStruct((slots, width + LANES), jnp.bfloat16),
        in_specs=[pl.BlockSpec(memory_space=VMEM)] * 4,
        out_specs=pl.BlockSpec(memory_space=VMEM),
        compiler_params=pltpu.CompilerParams(vmem_limit_bytes=24 * MIB),
        name="pool",
    )(counts, seg, rows, feats)


def pick_kernel(got_ref, out_ref, *, cards, cap, groups):
    senders, slots, wide = got_ref.shape
    width = wide - LANES
    total = senders * slots
    got = got_ref[...].reshape(total, wide)
    label = got[:, width : width + 1].astype(jnp.float32).astype(jnp.int32)
    slot = lax.broadcasted_iota(jnp.int32, (total, 1), 0)
    card = jnp.where(label >= 0, ((slot // cap) % groups) * cards + label, -1)
    ids = lax.broadcasted_iota(jnp.int32, (total, groups * cards), 1)
    hot = (ids == card).astype(jnp.float32).astype(jnp.bfloat16)
    out = lax.dot_general(
        hot, got[:, :width], (((0,), (0,)), ((), ())), preferred_element_type=jnp.float32
    )
    out_ref[...] = out.astype(jnp.bfloat16)


def pick(got, cap, groups):
    width = got.shape[2] - LANES
    out = pl.pallas_call(
        functools.partial(pick_kernel, cards=CARD_DEV, cap=cap, groups=groups),
        out_shape=jax.ShapeDtypeStruct((groups * CARD_DEV, width), jnp.bfloat16),
        in_specs=[pl.BlockSpec(memory_space=VMEM)],
        out_specs=pl.BlockSpec(memory_space=VMEM),
        compiler_params=pltpu.CompilerParams(vmem_limit_bytes=24 * MIB),
        name="pick",
    )(got)
    return out.reshape(groups, CARD_DEV, width)


def start_layer(out_ref, gain_ref, normed_ref, layer):
    u = out_ref[...].astype(jnp.float32)
    mean_sq = jnp.mean(u * u, axis=-1, keepdims=True)
    normed = u * lax.rsqrt(mean_sq + 1e-05) * gain_ref[pl.ds(layer, 1), :]
    normed_ref[...] = normed.astype(jnp.bfloat16)


def add_columns(out_ref, weight_ref, normed_ref, layer, block):
    width = out_ref.shape[1]
    columns = pl.ds(pl.multiple_of(block * BLOCK, BLOCK), BLOCK)
    y = jnp.dot(
        normed_ref[...],
        weight_ref[:, layer, :, columns].reshape(width, BLOCK),
        preferred_element_type=jnp.float32,
    )
    u = out_ref[:, columns].astype(jnp.float32)
    out_ref[:, columns] = (u + y / (1.0 + jnp.exp(-y))).astype(jnp.bfloat16)


def run_layers(out_ref, gain_ref, weight_ref, normed_ref):
    def layer_of(layer, carry):
        start_layer(out_ref, gain_ref, normed_ref, layer)

        def columns_of(block, carry):
            add_columns(out_ref, weight_ref, normed_ref, layer, block)
            return carry

        return lax.fori_loop(0, out_ref.shape[1] // BLOCK, columns_of, carry)

    lax.fori_loop(0, weight_ref.shape[1], layer_of, 0)


def first_kernel(
    position_ref, queue_ref, gain_ref, gathered_ref, out_ref, weight_ref, normed_ref, sem, *, fresh
):
    layers = gathered_ref.shape[1]
    blocks = out_ref.shape[1] // BLOCK

    def copy_of(layer, block):
        columns = pl.ds(block * BLOCK, BLOCK)
        return pltpu.make_async_copy(
            gathered_ref.at[:, layer, :, columns],
            weight_ref.at[:, layer, :, columns],
            sem.at[layer, block],
        )

    copies = [[copy_of(layer, block) for block in range(blocks)] for layer in range(layers)]
    for row in copies:
        for copy in row:
            copy.start()
    active = position_ref[0] == 0

    @pl.when(active)
    def _():
        out_ref[...] = queue_ref[fresh : fresh + BATCH, :]
        for layer in range(layers):
            start_layer(out_ref, gain_ref, normed_ref, layer)
            for block in range(blocks):
                copies[layer][block].wait()
                add_columns(out_ref, weight_ref, normed_ref, layer, block)

    @pl.when(jnp.logical_not(active))
    def _():
        for row in copies:
            for copy in row:
                copy.wait()


def first_stage(position, queue, gain, gathered, fresh):
    shape = (BATCH, gain.shape[1])
    return pl.pallas_call(
        functools.partial(first_kernel, fresh=fresh),
        out_shape=(
            jax.ShapeDtypeStruct(shape, jnp.bfloat16),
            pltpu.VMEM(gathered.shape, jnp.bfloat16),
        ),
        in_specs=[pl.BlockSpec(memory_space=SMEM)]
        + [pl.BlockSpec(memory_space=VMEM)] * 2
        + [pl.BlockSpec(memory_space=pltpu.MemorySpace.HBM)],
        out_specs=(pl.BlockSpec(memory_space=VMEM),) * 2,
        scratch_shapes=[
            pltpu.VMEM(shape, jnp.bfloat16),
            pltpu.SemaphoreType.DMA((gathered.shape[1], gain.shape[1] // BLOCK)),
        ],
        compiler_params=pltpu.CompilerParams(vmem_limit_bytes=24 * MIB),
        name="first_stage",
    )(position, queue, gain, pltpu.with_memory_space_constraint(gathered, pltpu.MemorySpace.HBM))


def stage_kernel(position_ref, *refs, step, fresh):
    *sources, gain_ref, weight_ref, out_ref, normed_ref = refs
    age = step - position_ref[0]

    @pl.when((age >= 0) & (age < TURNS))
    def _():
        if fresh is None:
            out_ref[...] = sources[-1][...]
        elif len(sources) == 1:
            out_ref[...] = sources[0][fresh : fresh + BATCH, :]
        else:
            first = position_ref[0] == 0

            @pl.when(first)
            def _():
                out_ref[...] = sources[0][fresh : fresh + BATCH, :]

            @pl.when(jnp.logical_not(first))
            def _():
                out_ref[...] = sources[1][...]

        run_layers(out_ref, gain_ref, weight_ref, normed_ref)


def stage(position, queue, came, gain, weight, step, fresh):
    sources = [a for a in (queue if fresh is not None else None, came) if a is not None]
    shape = (BATCH, gain.shape[1])
    return pl.pallas_call(
        functools.partial(stage_kernel, step=step, fresh=fresh),
        out_shape=jax.ShapeDtypeStruct(shape, jnp.bfloat16),
        in_specs=[pl.BlockSpec(memory_space=SMEM)]
        + [pl.BlockSpec(memory_space=VMEM)] * (len(sources) + 2),
        out_specs=pl.BlockSpec(memory_space=VMEM),
        scratch_shapes=[pltpu.VMEM(shape, jnp.bfloat16)],
        compiler_params=pltpu.CompilerParams(vmem_limit_bytes=24 * MIB),
        name="stage",
    )(position, *sources, gain, weight)


def choose_kernel(position_ref, *refs, cases):
    out_ref = refs[-1]
    for homes, which, row in cases:
        mine = position_ref[0] == homes[0]
        for home in homes[1:]:
            mine = mine | (position_ref[0] == home)

        @pl.when(mine)
        def _():
            out_ref[...] = refs[which][row : row + CARD_DEV, :]


def choose(position, arrays, cases):
    return pl.pallas_call(
        functools.partial(choose_kernel, cases=cases),
        out_shape=jax.ShapeDtypeStruct((CARD_DEV, arrays[0].shape[1]), jnp.bfloat16),
        in_specs=[pl.BlockSpec(memory_space=SMEM)]
        + [pl.BlockSpec(memory_space=VMEM)] * len(arrays),
        out_specs=pl.BlockSpec(memory_space=VMEM),
        compiler_params=pltpu.CompilerParams(vmem_limit_bytes=8 * MIB),
        name="choose",
    )(position, *arrays)


def collect(pooled):
    pairs = jnp.concatenate([lax.ppermute(pooled, "z", [(7, 0), (1, 2), (3, 4), (5, 6)]), pooled])
    fours = jnp.concatenate([pairs, lax.ppermute(pairs, "z", [(2, 0), (6, 4)])])
    return jnp.concatenate([fours, lax.ppermute(fours, "z", [(4, 0)])])


def crossing(moves):
    return [(C * a + c, C * b + C - 1 - c) for a, b in moves for c in range(C)]


def tower(position, queue, gain, gathered):
    streams = [
        dict(fresh=(2 * CARD_DEV, 6 * CARD_DEV), home=(2, 6)),
        dict(fresh=(4 * CARD_DEV, 0), home=(4, 0)),
    ]
    came = [None, None]
    kept = [[], []]
    done = [None, None]
    for step in range(Z - 1 + TURNS):
        for s, stream in enumerate(streams):
            fresh = stream["fresh"][step] if step < TURNS else None
            if step == 0 and s == 0:
                done[s], weight = first_stage(position, queue, gain, gathered, fresh)
            else:
                done[s] = stage(position, queue, came[s], gain, weight, step, fresh)
            moves = [(z, z + 1) for z in range(Z - 1) if 0 <= step - z < TURNS]
            if step >= Z - 1:
                moves.append((Z - 1, stream["home"][step - Z + 1]))
            came[s] = lax.ppermute(done[s], ("z", "c"), crossing(moves))
            if step >= Z - 1:
                kept[s].append(came[s])
    (two, six), (four, zero) = kept
    lent = choose(
        position,
        [two, four, six, done[1]],
        (((2,), 0, 0), ((4,), 1, 0), ((6,), 2, 0), ((Z - 1,), 3, 0)),
    )
    straight = [(C * a + c, C * b + c) for a, b in ((2, 1), (4, 3), (6, 5)) for c in range(C)]
    lent = lax.ppermute(lent, ("z", "c"), straight + crossing([(Z - 1, Z - 1)]))
    cases = (
        ((2,), 0, CARD_DEV),
        ((4,), 1, CARD_DEV),
        ((6,), 2, CARD_DEV),
        ((0,), 3, CARD_DEV),
        ((1, 3, 5, 7), 4, 0),
    )
    return choose(position, [two, four, six, zero, lent], cases)


def body(txn_feats, txn_seg, seg_row, send_counts, gains, tower_w):
    width = txn_feats.shape[1]
    slots = seg_row.shape[1]
    cap = slots // (X * Y)
    gathered = lax.all_gather(tower_w[0], ("x", "y", "c"), axis=0, tiled=False)
    gain = lax.all_gather(gains[0], "c", axis=0, tiled=False)
    buffer = pool(send_counts, txn_seg, seg_row, txn_feats)
    got = lax.all_to_all(buffer.reshape(X, Y * cap, width + LANES), "x", 0, 0, tiled=True)
    dense = pick(got, cap, Y)
    shares = lax.all_to_all(dense, "y", 0, 0, tiled=True)
    pooled = jnp.sum(shares.astype(jnp.float32), axis=0).astype(jnp.bfloat16)
    queue = collect(pooled)
    weight = gathered.reshape(X * Y, C, *tower_w.shape[1:])
    position = lax.axis_index("z").reshape(1)
    return tower(position, queue, gain, weight)


def solution(mesh):
    split = Mesh(mesh.devices.reshape(X, Y, Z, C), DEVICES)
    in_specs = (
        P(DEVICES, None),
        P(DEVICES, None),
        P(DEVICES, None),
        P(DEVICES, None),
        P(("z", "c"), None),
        P(("z", "c"), ("x", "y"), None),
    )
    return jax.shard_map(
        body, mesh=split, in_specs=in_specs, out_specs=P(DEVICES, None), check_vma=False
    )
```

```python
import functools

import jax
import jax.numpy as jnp
from jax import lax
from jax.experimental import pallas as pl
from jax.experimental.pallas import tpu as pltpu
from jax.sharding import Mesh, PartitionSpec as P

CARD_DEV = 16
X, Y, Z, C = 4, 8, 8, 2
DEVICES = ("x", "y", "z", "c")
LANES = 128
BLOCK = 1024
TURNS = 2
BATCH = 2 * CARD_DEV
VMEM = pltpu.MemorySpace.VMEM
SMEM = pltpu.MemorySpace.SMEM
MIB = 1024 * 1024


def pool_kernel(counts_ref, seg_ref, rows_ref, feats_ref, out_ref, *, cap):
    owners = counts_ref.shape[1]
    slots = rows_ref.shape[1]
    txns, width = feats_ref.shape
    counts = counts_ref[...]
    below = lax.broadcasted_iota(jnp.int32, (owners, owners), 0)
    across = lax.broadcasted_iota(jnp.int32, (owners, owners), 1)
    counts_all = jnp.broadcast_to(counts, (owners, owners))
    starts_col = jnp.sum(jnp.where(across < below, counts_all, 0), axis=1, keepdims=True)
    counts_col = jnp.sum(jnp.where(across == below, counts_all, 0), axis=1, keepdims=True)
    ends_col = starts_col + counts_col
    starts_row = jnp.sum(
        jnp.where(below < across, jnp.broadcast_to(counts_col, (owners, owners)), 0),
        axis=0,
        keepdims=True,
    )
    seg = seg_ref[...]
    ids = lax.broadcasted_iota(jnp.int32, (owners, txns), 0)
    owner = jnp.sum((seg >= ends_col).astype(jnp.int32), axis=0, keepdims=True)
    start = jnp.sum(jnp.where(ids == owner, starts_col, 0), axis=0, keepdims=True)
    target = owner * cap + seg - start
    slot = lax.broadcasted_iota(jnp.int32, (slots, txns), 0)
    place = (slot == target).astype(jnp.float32).astype(jnp.bfloat16)
    part = jnp.dot(place, feats_ref[...], preferred_element_type=jnp.float32)
    out_ref[:, :width] = part.astype(jnp.bfloat16)
    slot_col = lax.broadcasted_iota(jnp.int32, (slots, owners), 0)
    owner_row = lax.broadcasted_iota(jnp.int32, (slots, owners), 1)
    mine = (slot_col // cap) == owner_row
    slot_start = jnp.sum(jnp.where(mine, starts_row, 0), axis=1, keepdims=True)
    slot_count = jnp.sum(jnp.where(mine, counts, 0), axis=1, keepdims=True)
    rank = lax.broadcasted_iota(jnp.int32, (slots, 1), 0) % cap
    named = lax.broadcasted_iota(jnp.int32, (slots, slots), 1) == slot_start + rank
    row = jnp.sum(jnp.where(named, rows_ref[...], 0), axis=1, keepdims=True)
    label = jnp.where(rank < slot_count, row, -1)
    out_ref[:, width:] = jnp.broadcast_to(
        label.astype(jnp.float32), (slots, LANES)
    ).astype(jnp.bfloat16)


def pool(counts, seg, rows, feats):
    slots = rows.shape[1]
    width = feats.shape[1]
    cap = slots // counts.shape[1]
    return pl.pallas_call(
        functools.partial(pool_kernel, cap=cap),
        out_shape=jax.ShapeDtypeStruct((slots, width + LANES), jnp.bfloat16),
        in_specs=[pl.BlockSpec(memory_space=VMEM)] * 4,
        out_specs=pl.BlockSpec(memory_space=VMEM),
        compiler_params=pltpu.CompilerParams(vmem_limit_bytes=24 * MIB),
        name="pool",
    )(counts, seg, rows, feats)


def pick_kernel(got_ref, out_ref, *, cards, cap, groups):
    senders, slots, wide = got_ref.shape
    width = wide - LANES
    total = senders * slots
    got = got_ref[...].reshape(total, wide)
    label = got[:, width : width + 1].astype(jnp.float32).astype(jnp.int32)
    slot = lax.broadcasted_iota(jnp.int32, (total, 1), 0)
    card = jnp.where(label >= 0, ((slot // cap) % groups) * cards + label, -1)
    ids = lax.broadcasted_iota(jnp.int32, (total, groups * cards), 1)
    hot = (ids == card).astype(jnp.float32).astype(jnp.bfloat16)
    out = lax.dot_general(
        hot, got[:, :width], (((0,), (0,)), ((), ())), preferred_element_type=jnp.float32
    )
    out_ref[...] = out.astype(jnp.bfloat16)


def pick(got, cap, groups):
    width = got.shape[2] - LANES
    out = pl.pallas_call(
        functools.partial(pick_kernel, cards=CARD_DEV, cap=cap, groups=groups),
        out_shape=jax.ShapeDtypeStruct((groups * CARD_DEV, width), jnp.bfloat16),
        in_specs=[pl.BlockSpec(memory_space=VMEM)],
        out_specs=pl.BlockSpec(memory_space=VMEM),
        compiler_params=pltpu.CompilerParams(vmem_limit_bytes=24 * MIB),
        name="pick",
    )(got)
    return out.reshape(groups, CARD_DEV, width)


def start_layer(out_ref, gain_ref, normed_ref, layer):
    u = out_ref[...].astype(jnp.float32)
    mean_sq = jnp.mean(u * u, axis=-1, keepdims=True)
    normed = u * lax.rsqrt(mean_sq + 1e-05) * gain_ref[pl.ds(layer, 1), :]
    normed_ref[...] = normed.astype(jnp.bfloat16)


def add_columns(out_ref, weight_ref, normed_ref, layer, block):
    width = out_ref.shape[1]
    columns = pl.ds(pl.multiple_of(block * BLOCK, BLOCK), BLOCK)
    y = jnp.dot(
        normed_ref[...],
        weight_ref[:, layer, :, columns].reshape(width, BLOCK),
        preferred_element_type=jnp.float32,
    )
    u = out_ref[:, columns].astype(jnp.float32)
    out_ref[:, columns] = (u + y / (1.0 + jnp.exp(-y))).astype(jnp.bfloat16)


def run_layers(out_ref, gain_ref, weight_ref, normed_ref):
    def layer_of(layer, carry):
        start_layer(out_ref, gain_ref, normed_ref, layer)

        def columns_of(block, carry):
            add_columns(out_ref, weight_ref, normed_ref, layer, block)
            return carry

        return lax.fori_loop(0, out_ref.shape[1] // BLOCK, columns_of, carry)

    lax.fori_loop(0, weight_ref.shape[1], layer_of, 0)


def first_kernel(
    position_ref, queue_ref, gain_ref, gathered_ref, out_ref, weight_ref, normed_ref, sem, *, fresh
):
    layers = gathered_ref.shape[1]
    blocks = out_ref.shape[1] // BLOCK

    def copy_of(layer, block):
        columns = pl.ds(block * BLOCK, BLOCK)
        return pltpu.make_async_copy(
            gathered_ref.at[:, layer, :, columns],
            weight_ref.at[:, layer, :, columns],
            sem.at[layer, block],
        )

    copies = [[copy_of(layer, block) for block in range(blocks)] for layer in range(layers)]
    for row in copies:
        for copy in row:
            copy.start()
    active = position_ref[0] == 0

    @pl.when(active)
    def _():
        out_ref[...] = queue_ref[fresh : fresh + BATCH, :]
        for layer in range(layers):
            start_layer(out_ref, gain_ref, normed_ref, layer)
            for block in range(blocks):
                copies[layer][block].wait()
                add_columns(out_ref, weight_ref, normed_ref, layer, block)

    @pl.when(jnp.logical_not(active))
    def _():
        for row in copies:
            for copy in row:
                copy.wait()


def first_stage(position, queue, gain, gathered, fresh):
    shape = (BATCH, gain.shape[1])
    return pl.pallas_call(
        functools.partial(first_kernel, fresh=fresh),
        out_shape=(
            jax.ShapeDtypeStruct(shape, jnp.bfloat16),
            pltpu.VMEM(gathered.shape, jnp.bfloat16),
        ),
        in_specs=[pl.BlockSpec(memory_space=SMEM)]
        + [pl.BlockSpec(memory_space=VMEM)] * 2
        + [pl.BlockSpec(memory_space=pltpu.MemorySpace.HBM)],
        out_specs=(pl.BlockSpec(memory_space=VMEM),) * 2,
        scratch_shapes=[
            pltpu.VMEM(shape, jnp.bfloat16),
            pltpu.SemaphoreType.DMA((gathered.shape[1], gain.shape[1] // BLOCK)),
        ],
        compiler_params=pltpu.CompilerParams(vmem_limit_bytes=24 * MIB),
        name="first_stage",
    )(position, queue, gain, pltpu.with_memory_space_constraint(gathered, pltpu.MemorySpace.HBM))


def stage_kernel(position_ref, *refs, step, fresh):
    *sources, gain_ref, weight_ref, out_ref, normed_ref = refs
    age = step - position_ref[0]

    @pl.when((age >= 0) & (age < TURNS))
    def _():
        if fresh is None:
            out_ref[...] = sources[-1][...]
        elif len(sources) == 1:
            out_ref[...] = sources[0][fresh : fresh + BATCH, :]
        else:
            first = position_ref[0] == 0

            @pl.when(first)
            def _():
                out_ref[...] = sources[0][fresh : fresh + BATCH, :]

            @pl.when(jnp.logical_not(first))
            def _():
                out_ref[...] = sources[1][...]

        run_layers(out_ref, gain_ref, weight_ref, normed_ref)


def stage(position, queue, came, gain, weight, step, fresh):
    sources = [a for a in (queue if fresh is not None else None, came) if a is not None]
    shape = (BATCH, gain.shape[1])
    return pl.pallas_call(
        functools.partial(stage_kernel, step=step, fresh=fresh),
        out_shape=jax.ShapeDtypeStruct(shape, jnp.bfloat16),
        in_specs=[pl.BlockSpec(memory_space=SMEM)]
        + [pl.BlockSpec(memory_space=VMEM)] * (len(sources) + 2),
        out_specs=pl.BlockSpec(memory_space=VMEM),
        scratch_shapes=[pltpu.VMEM(shape, jnp.bfloat16)],
        compiler_params=pltpu.CompilerParams(vmem_limit_bytes=24 * MIB),
        name="stage",
    )(position, *sources, gain, weight)


def choose_kernel(position_ref, *refs, cases):
    out_ref = refs[-1]
    for homes, which, row in cases:
        mine = position_ref[0] == homes[0]
        for home in homes[1:]:
            mine = mine | (position_ref[0] == home)

        @pl.when(mine)
        def _():
            out_ref[...] = refs[which][row : row + CARD_DEV, :]


def choose(position, arrays, cases):
    return pl.pallas_call(
        functools.partial(choose_kernel, cases=cases),
        out_shape=jax.ShapeDtypeStruct((CARD_DEV, arrays[0].shape[1]), jnp.bfloat16),
        in_specs=[pl.BlockSpec(memory_space=SMEM)]
        + [pl.BlockSpec(memory_space=VMEM)] * len(arrays),
        out_specs=pl.BlockSpec(memory_space=VMEM),
        compiler_params=pltpu.CompilerParams(vmem_limit_bytes=8 * MIB),
        name="choose",
    )(position, *arrays)


def collect(pooled):
    pairs = jnp.concatenate([lax.ppermute(pooled, "z", [(7, 0), (1, 2), (3, 4), (5, 6)]), pooled])
    fours = jnp.concatenate([pairs, lax.ppermute(pairs, "z", [(2, 0), (6, 4)])])
    return jnp.concatenate([fours, lax.ppermute(fours, "z", [(4, 0)])])


def tower(position, queue, gain, gathered):
    streams = [
        dict(fresh=(2 * CARD_DEV, 6 * CARD_DEV), home=(2, 6)),
        dict(fresh=(4 * CARD_DEV, 0), home=(4, 0)),
    ]
    came = [None, None]
    kept = [[], []]
    done = [None, None]
    for step in range(Z - 1 + TURNS):
        for s, stream in enumerate(streams):
            fresh = stream["fresh"][step] if step < TURNS else None
            if step == 0 and s == 0:
                done[s], weight = first_stage(position, queue, gain, gathered, fresh)
            else:
                done[s] = stage(position, queue, came[s], gain, weight, step, fresh)
            moves = [(z, z + 1) for z in range(Z - 1) if 0 <= step - z < TURNS]
            if step >= Z - 1:
                moves.append((Z - 1, stream["home"][step - Z + 1]))
            came[s] = lax.ppermute(done[s], "z", moves)
            if step >= Z - 1:
                kept[s].append(came[s])
    (two, six), (four, zero) = kept
    lent = choose(position, [two, four, six], (((2,), 0, 0), ((4,), 1, 0), ((6,), 2, 0)))
    lent = lax.ppermute(lent, "z", [(2, 1), (4, 3), (6, 5)])
    cases = (
        ((2,), 0, CARD_DEV),
        ((4,), 1, CARD_DEV),
        ((6,), 2, CARD_DEV),
        ((0,), 3, CARD_DEV),
        ((1, 3, 5), 4, 0),
        ((7,), 5, 0),
    )
    return choose(position, [two, four, six, zero, lent, done[1]], cases)


def body(txn_feats, txn_seg, seg_row, send_counts, gains, tower_w):
    width = txn_feats.shape[1]
    slots = seg_row.shape[1]
    cap = slots // (X * Y)
    gathered = lax.all_gather(tower_w[0], ("x", "y", "c"), axis=0, tiled=False)
    gain = lax.all_gather(gains[0], "c", axis=0, tiled=False)
    buffer = pool(send_counts, txn_seg, seg_row, txn_feats)
    got = lax.all_to_all(buffer.reshape(X, Y * cap, width + LANES), "x", 0, 0, tiled=True)
    dense = pick(got, cap, Y)
    shares = lax.all_to_all(dense, "y", 0, 0, tiled=True)
    pooled = jnp.sum(shares.astype(jnp.float32), axis=0).astype(jnp.bfloat16)
    queue = collect(pooled)
    weight = gathered.reshape(X * Y, C, *tower_w.shape[1:])
    position = lax.axis_index("z").reshape(1)
    return tower(position, queue, gain, weight)


def solution(mesh):
    split = Mesh(mesh.devices.reshape(X, Y, Z, C), DEVICES)
    in_specs = (
        P(DEVICES, None),
        P(DEVICES, None),
        P(DEVICES, None),
        P(DEVICES, None),
        P(("z", "c"), None),
        P(("z", "c"), ("x", "y"), None),
    )
    return jax.shard_map(
        body, mesh=split, in_specs=in_specs, out_specs=P(DEVICES, None), check_vma=False
    )
```

```python
import functools

import jax
import jax.numpy as jnp
from jax import lax
from jax.experimental import pallas as pl
from jax.experimental.pallas import tpu as pltpu
from jax.sharding import Mesh, PartitionSpec as P

CARD_DEV = 16
X, Y, Z, C = 4, 8, 8, 2
DEVICES = ("x", "y", "z", "c")
LANES = 128
BLOCK = 1024
TURNS = 2
BATCH = 2 * CARD_DEV
VMEM = pltpu.MemorySpace.VMEM
SMEM = pltpu.MemorySpace.SMEM
MIB = 1024 * 1024


def pool_kernel(counts_ref, seg_ref, rows_ref, feats_ref, out_ref, *, cap):
    owners = counts_ref.shape[1]
    slots = rows_ref.shape[1]
    txns, width = feats_ref.shape
    counts = counts_ref[...]
    below = lax.broadcasted_iota(jnp.int32, (owners, owners), 0)
    across = lax.broadcasted_iota(jnp.int32, (owners, owners), 1)
    counts_all = jnp.broadcast_to(counts, (owners, owners))
    starts_col = jnp.sum(jnp.where(across < below, counts_all, 0), axis=1, keepdims=True)
    counts_col = jnp.sum(jnp.where(across == below, counts_all, 0), axis=1, keepdims=True)
    ends_col = starts_col + counts_col
    starts_row = jnp.sum(
        jnp.where(below < across, jnp.broadcast_to(counts_col, (owners, owners)), 0),
        axis=0,
        keepdims=True,
    )
    seg = seg_ref[...]
    ids = lax.broadcasted_iota(jnp.int32, (owners, txns), 0)
    owner = jnp.sum((seg >= ends_col).astype(jnp.int32), axis=0, keepdims=True)
    start = jnp.sum(jnp.where(ids == owner, starts_col, 0), axis=0, keepdims=True)
    target = owner * cap + seg - start
    slot = lax.broadcasted_iota(jnp.int32, (slots, txns), 0)
    place = (slot == target).astype(jnp.float32).astype(jnp.bfloat16)
    part = jnp.dot(place, feats_ref[...], preferred_element_type=jnp.float32)
    out_ref[:, :width] = part.astype(jnp.bfloat16)
    slot_col = lax.broadcasted_iota(jnp.int32, (slots, owners), 0)
    owner_row = lax.broadcasted_iota(jnp.int32, (slots, owners), 1)
    mine = (slot_col // cap) == owner_row
    slot_start = jnp.sum(jnp.where(mine, starts_row, 0), axis=1, keepdims=True)
    slot_count = jnp.sum(jnp.where(mine, counts, 0), axis=1, keepdims=True)
    rank = lax.broadcasted_iota(jnp.int32, (slots, 1), 0) % cap
    named = lax.broadcasted_iota(jnp.int32, (slots, slots), 1) == slot_start + rank
    row = jnp.sum(jnp.where(named, rows_ref[...], 0), axis=1, keepdims=True)
    label = jnp.where(rank < slot_count, row, -1)
    out_ref[:, width:] = jnp.broadcast_to(
        label.astype(jnp.float32), (slots, LANES)
    ).astype(jnp.bfloat16)


def pool(counts, seg, rows, feats):
    slots = rows.shape[1]
    width = feats.shape[1]
    cap = slots // counts.shape[1]
    return pl.pallas_call(
        functools.partial(pool_kernel, cap=cap),
        out_shape=jax.ShapeDtypeStruct((slots, width + LANES), jnp.bfloat16),
        in_specs=[pl.BlockSpec(memory_space=VMEM)] * 4,
        out_specs=pl.BlockSpec(memory_space=VMEM),
        compiler_params=pltpu.CompilerParams(vmem_limit_bytes=24 * MIB),
        name="pool",
    )(counts, seg, rows, feats)


def pick_kernel(got_ref, out_ref, *, cards, cap, groups):
    senders, slots, wide = got_ref.shape
    width = wide - LANES
    total = senders * slots
    got = got_ref[...].reshape(total, wide)
    label = got[:, width : width + 1].astype(jnp.float32).astype(jnp.int32)
    slot = lax.broadcasted_iota(jnp.int32, (total, 1), 0)
    card = jnp.where(label >= 0, ((slot // cap) % groups) * cards + label, -1)
    ids = lax.broadcasted_iota(jnp.int32, (total, groups * cards), 1)
    hot = (ids == card).astype(jnp.float32).astype(jnp.bfloat16)
    out = lax.dot_general(
        hot, got[:, :width], (((0,), (0,)), ((), ())), preferred_element_type=jnp.float32
    )
    out_ref[...] = out.astype(jnp.bfloat16)


def pick(got, cap, groups):
    width = got.shape[2] - LANES
    out = pl.pallas_call(
        functools.partial(pick_kernel, cards=CARD_DEV, cap=cap, groups=groups),
        out_shape=jax.ShapeDtypeStruct((groups * CARD_DEV, width), jnp.bfloat16),
        in_specs=[pl.BlockSpec(memory_space=VMEM)],
        out_specs=pl.BlockSpec(memory_space=VMEM),
        compiler_params=pltpu.CompilerParams(vmem_limit_bytes=24 * MIB),
        name="pick",
    )(got)
    return out.reshape(groups, CARD_DEV, width)


def start_layer(out_ref, gain_ref, normed_ref, layer):
    u = out_ref[...].astype(jnp.float32)
    mean_sq = jnp.mean(u * u, axis=-1, keepdims=True)
    normed = u * lax.rsqrt(mean_sq + 1e-05) * gain_ref[pl.ds(layer, 1), :]
    normed_ref[...] = normed.astype(jnp.bfloat16)


def add_columns(out_ref, weight_ref, normed_ref, layer, block):
    width = out_ref.shape[1]
    columns = pl.ds(pl.multiple_of(block * BLOCK, BLOCK), BLOCK)
    y = jnp.dot(
        normed_ref[...],
        weight_ref[:, layer, :, columns].reshape(width, BLOCK),
        preferred_element_type=jnp.float32,
    )
    u = out_ref[:, columns].astype(jnp.float32)
    out_ref[:, columns] = (u + y / (1.0 + jnp.exp(-y))).astype(jnp.bfloat16)


def run_layers(out_ref, gain_ref, weight_ref, normed_ref):
    def layer_of(layer, carry):
        start_layer(out_ref, gain_ref, normed_ref, layer)

        def columns_of(block, carry):
            add_columns(out_ref, weight_ref, normed_ref, layer, block)
            return carry

        return lax.fori_loop(0, out_ref.shape[1] // BLOCK, columns_of, carry)

    lax.fori_loop(0, weight_ref.shape[1], layer_of, 0)


def first_kernel(
    position_ref, queue_ref, gain_ref, gathered_ref, out_ref, weight_ref, normed_ref, sem, *, fresh
):
    layers = gathered_ref.shape[1]
    blocks = out_ref.shape[1] // BLOCK

    def copy_of(layer, block):
        columns = pl.ds(block * BLOCK, BLOCK)
        return pltpu.make_async_copy(
            gathered_ref.at[:, layer, :, columns],
            weight_ref.at[:, layer, :, columns],
            sem.at[layer, block],
        )

    copies = [[copy_of(layer, block) for block in range(blocks)] for layer in range(layers)]
    for row in copies:
        for copy in row:
            copy.start()
    active = position_ref[0] == 0

    @pl.when(active)
    def _():
        out_ref[...] = queue_ref[fresh : fresh + BATCH, :]
        for layer in range(layers):
            start_layer(out_ref, gain_ref, normed_ref, layer)
            for block in range(blocks):
                copies[layer][block].wait()
                add_columns(out_ref, weight_ref, normed_ref, layer, block)

    @pl.when(jnp.logical_not(active))
    def _():
        for row in copies:
            for copy in row:
                copy.wait()


def first_stage(position, queue, gain, gathered, fresh):
    shape = (BATCH, gain.shape[1])
    return pl.pallas_call(
        functools.partial(first_kernel, fresh=fresh),
        out_shape=(
            jax.ShapeDtypeStruct(shape, jnp.bfloat16),
            pltpu.VMEM(gathered.shape, jnp.bfloat16),
        ),
        in_specs=[pl.BlockSpec(memory_space=SMEM)]
        + [pl.BlockSpec(memory_space=VMEM)] * 2
        + [pl.BlockSpec(memory_space=pltpu.MemorySpace.HBM)],
        out_specs=(pl.BlockSpec(memory_space=VMEM),) * 2,
        scratch_shapes=[
            pltpu.VMEM(shape, jnp.bfloat16),
            pltpu.SemaphoreType.DMA((gathered.shape[1], gain.shape[1] // BLOCK)),
        ],
        compiler_params=pltpu.CompilerParams(vmem_limit_bytes=24 * MIB),
        name="first_stage",
    )(position, queue, gain, pltpu.with_memory_space_constraint(gathered, pltpu.MemorySpace.HBM))


def stage_kernel(position_ref, *refs, step, fresh):
    *sources, gain_ref, weight_ref, out_ref, normed_ref = refs
    age = step - position_ref[0]

    @pl.when((age >= 0) & (age < TURNS))
    def _():
        if fresh is None:
            out_ref[...] = sources[-1][...]
        elif len(sources) == 1:
            out_ref[...] = sources[0][fresh : fresh + BATCH, :]
        else:
            first = position_ref[0] == 0

            @pl.when(first)
            def _():
                out_ref[...] = sources[0][fresh : fresh + BATCH, :]

            @pl.when(jnp.logical_not(first))
            def _():
                out_ref[...] = sources[1][...]

        run_layers(out_ref, gain_ref, weight_ref, normed_ref)


def stage(position, queue, came, gain, weight, step, fresh, after):
    sources = [a for a in (queue if fresh is not None else after, came) if a is not None]
    shape = (BATCH, gain.shape[1])
    return pl.pallas_call(
        functools.partial(stage_kernel, step=step, fresh=fresh),
        out_shape=jax.ShapeDtypeStruct(shape, jnp.bfloat16),
        in_specs=[pl.BlockSpec(memory_space=SMEM)]
        + [pl.BlockSpec(memory_space=VMEM)] * (len(sources) + 2),
        out_specs=pl.BlockSpec(memory_space=VMEM),
        scratch_shapes=[pltpu.VMEM(shape, jnp.bfloat16)],
        compiler_params=pltpu.CompilerParams(vmem_limit_bytes=24 * MIB),
        name="stage",
    )(position, *sources, gain, weight)


def choose_kernel(position_ref, *refs, cases):
    out_ref = refs[-1]
    for homes, which, row in cases:
        mine = position_ref[0] == homes[0]
        for home in homes[1:]:
            mine = mine | (position_ref[0] == home)

        @pl.when(mine)
        def _():
            out_ref[...] = refs[which][row : row + CARD_DEV, :]


def choose(position, arrays, cases):
    return pl.pallas_call(
        functools.partial(choose_kernel, cases=cases),
        out_shape=jax.ShapeDtypeStruct((CARD_DEV, arrays[0].shape[1]), jnp.bfloat16),
        in_specs=[pl.BlockSpec(memory_space=SMEM)]
        + [pl.BlockSpec(memory_space=VMEM)] * len(arrays),
        out_specs=pl.BlockSpec(memory_space=VMEM),
        compiler_params=pltpu.CompilerParams(vmem_limit_bytes=8 * MIB),
        name="choose",
    )(position, *arrays)


def collect(pooled):
    pairs = jnp.concatenate([pooled, lax.ppermute(pooled, "z", [(1, 0), (3, 2), (5, 4), (7, 6)])])
    fours = jnp.concatenate([pairs, lax.ppermute(pairs, "z", [(2, 0), (6, 4)])])
    return jnp.concatenate([fours, lax.ppermute(fours, "z", [(4, 0)])])


def tower(position, queue, gain, gathered):
    streams = [
        dict(fresh=(0, 2 * BATCH), home=(0, 5)),
        dict(fresh=(BATCH, 3 * BATCH), home=(2, 6)),
    ]
    came = [None, None]
    kept = [[], []]
    done = [None, None]
    for step in range(Z - 1 + TURNS):
        for s, stream in enumerate(streams):
            fresh = stream["fresh"][step] if step < TURNS else None
            if step == 0 and s == 0:
                done[s], weight = first_stage(position, queue, gain, gathered, fresh)
            else:
                after = done[0] if s == 1 else None
                done[s] = stage(position, queue, came[s], gain, weight, step, fresh, after)
            moves = [(z, z + 1) for z in range(Z - 1) if 0 <= step - z < TURNS]
            if step >= Z - 1:
                moves.append((Z - 1, stream["home"][step - Z + 1]))
            came[s] = lax.ppermute(done[s], "z", moves)
            if step >= Z - 1:
                kept[s].append(came[s])
            if step == Z and s == 0:
                four = lax.ppermute(done[s], "z", [(Z - 1, 4)])
    (zero, five), (two, six) = kept
    lent = choose(position, [zero, two, four, five], (((0,), 0, CARD_DEV), ((2,), 1, CARD_DEV)))
    lent = lax.ppermute(lent, "z", [(0, 1), (2, 3)])
    cases = (
        ((0,), 0, 0),
        ((2,), 1, 0),
        ((4,), 2, 0),
        ((5,), 3, CARD_DEV),
        ((6,), 4, 0),
        ((1, 3), 5, 0),
        ((7,), 6, CARD_DEV),
    )
    return choose(position, [zero, two, four, five, six, lent, done[1]], cases)


def body(txn_feats, txn_seg, seg_row, send_counts, gains, tower_w):
    width = txn_feats.shape[1]
    slots = seg_row.shape[1]
    cap = slots // (X * Y)
    gathered = lax.all_gather(tower_w[0], ("x", "y", "c"), axis=0, tiled=False)
    gain = lax.all_gather(gains[0], "c", axis=0, tiled=False)
    buffer = pool(send_counts, txn_seg, seg_row, txn_feats)
    got = lax.all_to_all(buffer.reshape(X, Y * cap, width + LANES), "x", 0, 0, tiled=True)
    dense = pick(got, cap, Y)
    shares = lax.all_to_all(dense, "y", 0, 0, tiled=True)
    pooled = jnp.sum(shares.astype(jnp.float32), axis=0).astype(jnp.bfloat16)
    queue = collect(pooled)
    weight = gathered.reshape(X * Y, C, *tower_w.shape[1:])
    position = lax.axis_index("z").reshape(1)
    return tower(position, queue, gain, weight)


def solution(mesh):
    split = Mesh(mesh.devices.reshape(X, Y, Z, C), DEVICES)
    in_specs = (
        P(DEVICES, None),
        P(DEVICES, None),
        P(DEVICES, None),
        P(DEVICES, None),
        P(("z", "c"), None),
        P(("z", "c"), ("x", "y"), None),
    )
    return jax.shard_map(
        body, mesh=split, in_specs=in_specs, out_specs=P(DEVICES, None), check_vma=False
    )
```

```python
import functools

import jax
import jax.numpy as jnp
from jax import lax
from jax.experimental import pallas as pl
from jax.experimental.pallas import tpu as pltpu
from jax.sharding import Mesh, PartitionSpec as P

CARD_DEV = 16
X, Y, Z, C = 4, 8, 8, 2
DEVICES = ("x", "y", "z", "c")
LANES = 128
BLOCK = 2048
FIRST_BLOCK = 512
TURNS = 2
BATCH = 2 * CARD_DEV
VMEM = pltpu.MemorySpace.VMEM
SMEM = pltpu.MemorySpace.SMEM
MIB = 1024 * 1024


def pool_kernel(counts_ref, seg_ref, rows_ref, feats_ref, out_ref, *, cap):
    owners = counts_ref.shape[1]
    slots = rows_ref.shape[1]
    txns, width = feats_ref.shape
    counts = counts_ref[...]
    below = lax.broadcasted_iota(jnp.int32, (owners, owners), 0)
    across = lax.broadcasted_iota(jnp.int32, (owners, owners), 1)
    counts_all = jnp.broadcast_to(counts, (owners, owners))
    starts_col = jnp.sum(jnp.where(across < below, counts_all, 0), axis=1, keepdims=True)
    counts_col = jnp.sum(jnp.where(across == below, counts_all, 0), axis=1, keepdims=True)
    ends_col = starts_col + counts_col
    starts_row = jnp.sum(
        jnp.where(below < across, jnp.broadcast_to(counts_col, (owners, owners)), 0),
        axis=0,
        keepdims=True,
    )
    seg = seg_ref[...]
    ids = lax.broadcasted_iota(jnp.int32, (owners, txns), 0)
    owner = jnp.sum((seg >= ends_col).astype(jnp.int32), axis=0, keepdims=True)
    start = jnp.sum(jnp.where(ids == owner, starts_col, 0), axis=0, keepdims=True)
    target = owner * cap + seg - start
    slot = lax.broadcasted_iota(jnp.int32, (slots, txns), 0)
    place = (slot == target).astype(jnp.float32).astype(jnp.bfloat16)
    part = jnp.dot(place, feats_ref[...], preferred_element_type=jnp.float32)
    out_ref[:, :width] = part.astype(jnp.bfloat16)
    slot_col = lax.broadcasted_iota(jnp.int32, (slots, owners), 0)
    owner_row = lax.broadcasted_iota(jnp.int32, (slots, owners), 1)
    mine = (slot_col // cap) == owner_row
    slot_start = jnp.sum(jnp.where(mine, starts_row, 0), axis=1, keepdims=True)
    slot_count = jnp.sum(jnp.where(mine, counts, 0), axis=1, keepdims=True)
    rank = lax.broadcasted_iota(jnp.int32, (slots, 1), 0) % cap
    named = lax.broadcasted_iota(jnp.int32, (slots, slots), 1) == slot_start + rank
    row = jnp.sum(jnp.where(named, rows_ref[...], 0), axis=1, keepdims=True)
    label = jnp.where(rank < slot_count, row, -1)
    out_ref[:, width:] = jnp.broadcast_to(
        label.astype(jnp.float32), (slots, LANES)
    ).astype(jnp.bfloat16)


def pool(counts, seg, rows, feats):
    slots = rows.shape[1]
    width = feats.shape[1]
    cap = slots // counts.shape[1]
    return pl.pallas_call(
        functools.partial(pool_kernel, cap=cap),
        out_shape=jax.ShapeDtypeStruct((slots, width + LANES), jnp.bfloat16),
        in_specs=[pl.BlockSpec(memory_space=VMEM)] * 4,
        out_specs=pl.BlockSpec(memory_space=VMEM),
        compiler_params=pltpu.CompilerParams(vmem_limit_bytes=24 * MIB),
        name="pool",
    )(counts, seg, rows, feats)


def pick_kernel(got_ref, out_ref, *, cards, cap, groups):
    senders, slots, wide = got_ref.shape
    width = wide - LANES
    total = senders * slots
    got = got_ref[...].reshape(total, wide)
    label = got[:, width : width + 1].astype(jnp.float32).astype(jnp.int32)
    slot = lax.broadcasted_iota(jnp.int32, (total, 1), 0)
    card = jnp.where(label >= 0, ((slot // cap) % groups) * cards + label, -1)
    ids = lax.broadcasted_iota(jnp.int32, (total, groups * cards), 1)
    hot = (ids == card).astype(jnp.float32).astype(jnp.bfloat16)
    out = lax.dot_general(
        hot, got[:, :width], (((0,), (0,)), ((), ())), preferred_element_type=jnp.float32
    )
    out_ref[...] = out.astype(jnp.bfloat16)


def pick(got, cap, groups):
    width = got.shape[2] - LANES
    out = pl.pallas_call(
        functools.partial(pick_kernel, cards=CARD_DEV, cap=cap, groups=groups),
        out_shape=jax.ShapeDtypeStruct((groups * CARD_DEV, width), jnp.bfloat16),
        in_specs=[pl.BlockSpec(memory_space=VMEM)],
        out_specs=pl.BlockSpec(memory_space=VMEM),
        compiler_params=pltpu.CompilerParams(vmem_limit_bytes=24 * MIB),
        name="pick",
    )(got)
    return out.reshape(groups, CARD_DEV, width)


def start_layer(out_ref, gain_ref, normed_ref, layer):
    u = out_ref[...].astype(jnp.float32)
    mean_sq = jnp.mean(u * u, axis=-1, keepdims=True)
    normed = u * lax.rsqrt(mean_sq + 1e-05) * gain_ref[pl.ds(layer, 1), :]
    normed_ref[...] = normed.astype(jnp.bfloat16)


def add_columns(out_ref, weight_ref, normed_ref, layer, block, size):
    width = out_ref.shape[1]
    columns = pl.ds(pl.multiple_of(block * size, size), size)
    y = jnp.dot(
        normed_ref[...],
        weight_ref[:, layer, :, columns].reshape(width, size),
        preferred_element_type=jnp.float32,
    )
    u = out_ref[:, columns].astype(jnp.float32)
    out_ref[:, columns] = (u + y / (1.0 + jnp.exp(-y))).astype(jnp.bfloat16)


def run_layers(out_ref, gain_ref, weight_ref, normed_ref):
    def layer_of(layer, carry):
        start_layer(out_ref, gain_ref, normed_ref, layer)

        def columns_of(block, carry):
            add_columns(out_ref, weight_ref, normed_ref, layer, block, BLOCK)
            return carry

        return lax.fori_loop(0, out_ref.shape[1] // BLOCK, columns_of, carry)

    lax.fori_loop(0, weight_ref.shape[1], layer_of, 0)


def first_kernel(
    position_ref, queue_ref, gain_ref, gathered_ref, out_ref, weight_ref, normed_ref, sem, *, fresh
):
    layers = gathered_ref.shape[1]
    blocks = out_ref.shape[1] // FIRST_BLOCK

    def copy_of(layer, block):
        columns = pl.ds(block * FIRST_BLOCK, FIRST_BLOCK)
        return pltpu.make_async_copy(
            gathered_ref.at[:, layer, :, columns],
            weight_ref.at[:, layer, :, columns],
            sem.at[layer, block],
        )

    copies = [[copy_of(layer, block) for block in range(blocks)] for layer in range(layers)]
    for row in copies:
        for copy in row:
            copy.start()
    active = position_ref[0] == 0

    @pl.when(active)
    def _():
        out_ref[...] = queue_ref[fresh : fresh + BATCH, :]
        for layer in range(layers):
            start_layer(out_ref, gain_ref, normed_ref, layer)
            for block in range(blocks):
                copies[layer][block].wait()
                add_columns(out_ref, weight_ref, normed_ref, layer, block, FIRST_BLOCK)

    @pl.when(jnp.logical_not(active))
    def _():
        for row in copies:
            for copy in row:
                copy.wait()


def first_stage(position, queue, gain, gathered, fresh):
    shape = (BATCH, gain.shape[1])
    return pl.pallas_call(
        functools.partial(first_kernel, fresh=fresh),
        out_shape=(
            jax.ShapeDtypeStruct(shape, jnp.bfloat16),
            pltpu.VMEM(gathered.shape, jnp.bfloat16),
        ),
        in_specs=[pl.BlockSpec(memory_space=SMEM)]
        + [pl.BlockSpec(memory_space=VMEM)] * 2
        + [pl.BlockSpec(memory_space=pltpu.MemorySpace.HBM)],
        out_specs=(pl.BlockSpec(memory_space=VMEM),) * 2,
        scratch_shapes=[
            pltpu.VMEM(shape, jnp.bfloat16),
            pltpu.SemaphoreType.DMA((gathered.shape[1], gain.shape[1] // FIRST_BLOCK)),
        ],
        compiler_params=pltpu.CompilerParams(vmem_limit_bytes=24 * MIB),
        name="first_stage",
    )(position, queue, gain, pltpu.with_memory_space_constraint(gathered, pltpu.MemorySpace.HBM))


def stage_kernel(position_ref, *refs, step, fresh):
    *sources, gain_ref, weight_ref, out_ref, normed_ref = refs
    age = step - position_ref[0]

    @pl.when((age >= 0) & (age < TURNS))
    def _():
        if fresh is None:
            out_ref[...] = sources[-1][...]
        elif len(sources) == 1:
            out_ref[...] = sources[0][fresh : fresh + BATCH, :]
        else:
            first = position_ref[0] == 0

            @pl.when(first)
            def _():
                out_ref[...] = sources[0][fresh : fresh + BATCH, :]

            @pl.when(jnp.logical_not(first))
            def _():
                out_ref[...] = sources[1][...]

        run_layers(out_ref, gain_ref, weight_ref, normed_ref)


def stage(position, queue, came, gain, weight, step, fresh, after):
    sources = [a for a in (queue if fresh is not None else after, came) if a is not None]
    shape = (BATCH, gain.shape[1])
    return pl.pallas_call(
        functools.partial(stage_kernel, step=step, fresh=fresh),
        out_shape=jax.ShapeDtypeStruct(shape, jnp.bfloat16),
        in_specs=[pl.BlockSpec(memory_space=SMEM)]
        + [pl.BlockSpec(memory_space=VMEM)] * (len(sources) + 2),
        out_specs=pl.BlockSpec(memory_space=VMEM),
        scratch_shapes=[pltpu.VMEM(shape, jnp.bfloat16)],
        compiler_params=pltpu.CompilerParams(
            vmem_limit_bytes=24 * MIB
        ),
        name="stage",
    )(position, *sources, gain, weight)


def choose_kernel(position_ref, *refs, cases):
    out_ref = refs[-1]
    for homes, which, row in cases:
        mine = position_ref[0] == homes[0]
        for home in homes[1:]:
            mine = mine | (position_ref[0] == home)

        @pl.when(mine)
        def _():
            out_ref[...] = refs[which][row : row + CARD_DEV, :]


def choose(position, arrays, cases):
    return pl.pallas_call(
        functools.partial(choose_kernel, cases=cases),
        out_shape=jax.ShapeDtypeStruct((CARD_DEV, arrays[0].shape[1]), jnp.bfloat16),
        in_specs=[pl.BlockSpec(memory_space=SMEM)]
        + [pl.BlockSpec(memory_space=VMEM)] * len(arrays),
        out_specs=pl.BlockSpec(memory_space=VMEM),
        compiler_params=pltpu.CompilerParams(vmem_limit_bytes=8 * MIB),
        name="choose",
    )(position, *arrays)


def collect(pooled):
    pairs = jnp.concatenate([pooled, lax.ppermute(pooled, "z", [(1, 0), (3, 2), (5, 4), (7, 6)])])
    fours = jnp.concatenate([pairs, lax.ppermute(pairs, "z", [(2, 0), (6, 4)])])
    return jnp.concatenate([fours, lax.ppermute(fours, "z", [(4, 0)])])


def tower(position, queue, gain, gathered):
    streams = [
        dict(fresh=(0, 2 * BATCH), home=(0, 5)),
        dict(fresh=(BATCH, 3 * BATCH), home=(2, 6)),
    ]
    came = [None, None]
    kept = [[], []]
    done = [None, None]
    for step in range(Z - 1 + TURNS):
        for s, stream in enumerate(streams):
            fresh = stream["fresh"][step] if step < TURNS else None
            if step == 0 and s == 0:
                done[s], weight = first_stage(position, queue, gain, gathered, fresh)
            else:
                after = done[0] if s == 1 else None
                done[s] = stage(position, queue, came[s], gain, weight, step, fresh, after)
            moves = [(z, z + 1) for z in range(Z - 1) if 0 <= step - z < TURNS]
            if step >= Z - 1:
                moves.append((Z - 1, stream["home"][step - Z + 1]))
            came[s] = lax.ppermute(done[s], "z", moves)
            if step >= Z - 1:
                kept[s].append(came[s])
            if step == Z and s == 0:
                four = lax.ppermute(done[s], "z", [(Z - 1, 4)])
    (zero, five), (two, six) = kept
    lent = choose(position, [zero, two, four, five], (((0,), 0, CARD_DEV), ((2,), 1, CARD_DEV)))
    lent = lax.ppermute(lent, "z", [(0, 1), (2, 3)])
    cases = (
        ((0,), 0, 0),
        ((2,), 1, 0),
        ((4,), 2, 0),
        ((5,), 3, CARD_DEV),
        ((6,), 4, 0),
        ((1, 3), 5, 0),
        ((7,), 6, CARD_DEV),
    )
    return choose(position, [zero, two, four, five, six, lent, done[1]], cases)


def body(txn_feats, txn_seg, seg_row, send_counts, gains, tower_w):
    width = txn_feats.shape[1]
    slots = seg_row.shape[1]
    cap = slots // (X * Y)
    gathered = lax.all_gather(tower_w[0], ("x", "y", "c"), axis=0, tiled=False)
    gain = lax.all_gather(gains[0], "c", axis=0, tiled=False)
    buffer = pool(send_counts, txn_seg, seg_row, txn_feats)
    got = lax.all_to_all(buffer.reshape(X, Y * cap, width + LANES), "x", 0, 0, tiled=True)
    dense = pick(got, cap, Y)
    shares = lax.all_to_all(dense, "y", 0, 0, tiled=True)
    pooled = jnp.sum(shares.astype(jnp.float32), axis=0).astype(jnp.bfloat16)
    queue = collect(pooled)
    weight = gathered.reshape(X * Y, C, *tower_w.shape[1:])
    position = lax.axis_index("z").reshape(1)
    return tower(position, queue, gain, weight)


def solution(mesh):
    split = Mesh(mesh.devices.reshape(X, Y, Z, C), DEVICES)
    in_specs = (
        P(DEVICES, None),
        P(DEVICES, None),
        P(DEVICES, None),
        P(DEVICES, None),
        P(("z", "c"), None),
        P(("z", "c"), ("x", "y"), None),
    )
    return jax.shard_map(
        body, mesh=split, in_specs=in_specs, out_specs=P(DEVICES, None), check_vma=False
    )
```
